32 devices in a mesh: tm: 4 (over z), tmpl: 8 (over y, x, core).
Axes of the slice: x: 2, y: 2, z: 4, core: 2. Of those that a mesh axis runs over, the one named last changes fastest.
Arguments:
- strain: float32 [8, 131072], P('tmpl', 'tm'), may hold values from -6 to 6
- psd_bins: int32 [4, 65536], P(None, 'tmpl'), may hold values from 0 to 8191, as said below
- psd_values: float32 [4, 8192], P('tm'), may hold values from 0.25 to 4
- chirp_slope: int32 [16], P('tmpl'), may hold values from 0 to 1023
- chirp_curve: int32 [16], P('tmpl'), may hold values from 1 to 63
Outputs:
- snr: float32 [16, 1048576], P('tmpl', 'tm')
The draws below stay inside these ranges and needn't reach their ends.
Inputs may be any that keep to these rules, and one draw needn't show every extreme that they name: psd_bins[r, c] names the row of psd_values that serves frequency bin r * 65536 + c.
All inputs are finite; a program needn't handle non-finite values.
Results may differ from the reference program's by a relative error of at most 0.0003.
Values sent between devices are 32-bit elements; how exact they have to be, the bound alone decides.
A program may use at most 128 MiB of HBM per device.

```python
import math
import jax
import jax.numpy as jnp
from jax import lax

SUB = 65536
OR = 32768
R = 8192
LANES = 8
SEGMENTS = 4
ROWS = 32768
HALF_ROWS = 4
TEMPLATES = 16


def draw_psd_bins(key, part):
    frequency = jnp.arange(HALF_ROWS * SUB, dtype=jnp.int32)
    base_row = frequency // (HALF_ROWS * SUB // R)
    jitter = jax.random.randint(key, frequency.shape, 0, 2, dtype=jnp.int32)
    jitter = jnp.where(frequency == 0, 0, jitter)
    return jnp.minimum(base_row + jitter, R - 1).reshape(HALF_ROWS, SUB)


def place_ends(entries, rng, smallest, high):
    extent = entries.shape
    spot = [jax.random.randint(jax.random.fold_in(rng, axis), (), 0, extent[axis]) for axis in range(len(extent))]
    entries = entries.at[tuple(spot)].set(smallest)
    longest = extent.index(max(extent))
    spot[longest] = (spot[longest] + 1) % extent[longest]
    return entries.at[tuple(spot)].set(high)


def block_scale(own_key, shape, pieces, smallest, largest):
    factor_of = 1.0
    for dim, shards_of in pieces:
        draws = jax.random.uniform(jax.random.fold_in(jax.random.fold_in(own_key, 6), dim), (shards_of,), jnp.float32, smallest / len(pieces), largest / len(pieces))
        factor_of = factor_of * jnp.repeat(jnp.exp(draws), shape[dim] // shards_of).reshape((-1,) + (1,) * (len(shape) - 1 - dim))
    return factor_of


def centred(key, shape, scale, bound, cuts=(), kind=jnp.bfloat16):
    loudness = block_scale(key, shape, cuts, -0.22, 0.18) if cuts else 1.0
    drawn = jax.random.normal(key, shape, jnp.float32) * scale * loudness
    return jnp.minimum(jnp.maximum(drawn, -bound), bound).astype(kind)


def setup_inputs(seed: int = 0) -> dict:
    splits = jax.random.split(jax.random.key(seed), 6)
    strain = centred(splits[0], (LANES, SEGMENTS * ROWS), 1.0, 6.0, ((0, 8), (1, 4)), jnp.float32)
    psd_bins = draw_psd_bins(jax.random.fold_in(splits[5], 71), 0)
    psd_values = jnp.clip(jnp.exp(math.log(4.0) - 2.7725887 * jax.random.uniform(splits[2], (SEGMENTS, R), jnp.float32) ** block_scale(splits[2], (SEGMENTS, R), ((0, 4),), -0.2, 0.2)), 0.25, 4.0)
    chirp_slope = place_ends(jax.random.randint(splits[3], (TEMPLATES,), 0, 1024), jax.random.fold_in(splits[3], 1), 0, 1023).astype(jnp.int32)
    chirp_curve = place_ends(jax.random.randint(splits[4], (TEMPLATES,), 1, 64), jax.random.fold_in(splits[4], 1), 1, 63).astype(jnp.int32)
    return {"strain": strain, "psd_bins": psd_bins, "psd_values": psd_values, "chirp_slope": chirp_slope, "chirp_curve": chirp_curve}


TWO_PI = 2.0 * math.pi

def chirp_phase(frequency, slope, curve, modulus):
    high_part = frequency // 1024
    low_part = frequency % 1024
    square = 2 * high_part * low_part % (modulus // 1024) * 1024 + low_part * low_part
    square = square % modulus
    return (slope * frequency + curve * square) % modulus

def template_parts(frequency, chirp_slope, chirp_curve, modulus, k_low, k_cut):
    phase = chirp_phase(frequency[None, :], chirp_slope[:, None], chirp_curve[:, None], modulus)
    angles = phase.astype(jnp.float32) * (TWO_PI / modulus)
    ratio = frequency.astype(jnp.float32) / k_low
    inside = (frequency >= k_low) & (frequency < k_cut)
    amplitude = jnp.where(inside, jnp.power(jnp.maximum(ratio, 1.0), -7.0 / 6.0), 0.0)
    return (amplitude * jnp.cos(angles), -amplitude * jnp.sin(angles))

def reference(strain, psd_bins, psd_values, chirp_slope, chirp_curve):
    lanes = strain.shape[0]
    total_len = SUB * lanes
    half_len = total_len // 2
    intersection = OR * lanes
    stride = ROWS * lanes
    stream = strain.T.reshape(-1)
    padded = jnp.concatenate([jnp.zeros((intersection,), jnp.float32), stream])
    frequency = jnp.arange(half_len, dtype=jnp.int32)
    tmpl_re, tmpl_im = template_parts(frequency, chirp_slope, chirp_curve, total_len, total_len // 200, 3 * total_len // 8)
    power = tmpl_re * tmpl_re + tmpl_im * tmpl_im
    bins = psd_bins.reshape(-1)
    norm_scale = 1.0 / math.sqrt(total_len)

    def one_segment(segment):
        start = (segment * stride).astype(jnp.int32)
        data = lax.dynamic_slice(padded, (start,), (total_len,))
        spectrum = jnp.fft.fft(data)[:half_len]
        inv_psd = 1.0 / jnp.take(psd_values[segment], bins)
        white_re = jnp.real(spectrum) * inv_psd * norm_scale
        white_im = jnp.imag(spectrum) * inv_psd * norm_scale
        coef_re = white_re * tmpl_re + white_im * tmpl_im
        coef_im = white_im * tmpl_re - white_re * tmpl_im
        widths = ((0, 0), (0, total_len - half_len))
        series = jnp.fft.ifft(lax.complex(jnp.pad(coef_re, widths), jnp.pad(coef_im, widths)), axis=-1) * total_len
        sigma_sq = lax.optimization_barrier(jnp.sum(power * inv_psd, axis=-1))
        magnitude = jnp.abs(series) / jnp.sqrt(sigma_sq)[:, None]
        return magnitude[:, intersection:]
    result = lax.map(one_segment, jnp.arange(SEGMENTS, dtype=jnp.int32))
    return jnp.transpose(result, (1, 0, 2)).reshape(result.shape[1], -1)
```

```python
import functools
import math

import jax
import jax.numpy as jnp
import numpy as np
from jax import lax
from jax.experimental import pallas as pl
from jax.experimental.pallas import tpu as pltpu
from jax.sharding import PartitionSpec as P

TWO_PI = 2.0 * math.pi
LANE = 128
FINE = 32
COARSE = 16
VMEM_LIMIT = 60 * 1024 * 1024
BF16 = jnp.bfloat16
F32 = jnp.float32
NN = (((1,), (0,)), ((), ()))
NT = (((1,), (1,)), ((), ()))


def shifted(block, axis, distance):
    devices = range(lax.axis_size(axis))
    route = [(i - distance, i) for i in devices if i - distance in devices]
    return lax.ppermute(block, axis, route)


def base_table(rows, cols, modulus, direction, start=0):
    first = start + FINE * np.arange(rows // FINE, dtype=np.int64)
    index = np.concatenate([first, np.arange(FINE, dtype=np.int64)])
    angle = (index[:, None] * np.asarray(cols, dtype=np.int64)[None, :] % modulus) * (
        direction * TWO_PI / modulus
    )
    return jnp.asarray(np.stack([np.cos(angle), np.sin(angle)]).astype(np.float32))


def product_rows(table, outer, coarse_count):
    c1 = table[0, pl.ds(outer, 1), :]
    s1 = table[1, pl.ds(outer, 1), :]
    c0 = table[0, coarse_count : coarse_count + FINE, :]
    s0 = table[1, coarse_count : coarse_count + FINE, :]
    return c1 * c0 - s1 * s0, s1 * c0 + c1 * s0


def halves(value):
    high = value.astype(BF16)
    return high, (value - high.astype(F32)).astype(BF16)


def put(ref, slot, index, value):
    high, low = halves(value)
    ref[(slot, 0) + index] = high
    ref[(slot, 1) + index] = low


def put_factor(ref, index, re, im):
    put(ref, 0, index, re)
    put(ref, 1, index, im - re)
    put(ref, 2, index, re + im)


def dot3(a, b, slot, dims):
    def one(i, j):
        return lax.dot_general(a[slot, i], b[slot, j], dims, preferred_element_type=F32)

    return one(0, 0) + (one(0, 1) + one(1, 0))


def complex_dot(a, b, dims):
    k1 = dot3(a, b, 0, dims)
    k2 = dot3(a, b, 1, dims)
    k3 = dot3(a, b, 2, dims)
    return k1 - k3, k1 + k2


def inverse_density(bins_ref, table_ref, out_ref):
    rows = bins_ref.shape[0]
    step = next(n for n in (64, 48, 32, 24, 16, 8) if rows % n == 0)
    for first in range(0, rows, step):
        bins = bins_ref[first : first + step, :]
        high = bins // LANE
        low = bins % LANE

        def body(row, total):
            line = jnp.broadcast_to(table_ref[pl.ds(row, 1), :], (step, LANE))
            return jnp.where(
                high == row,
                jnp.take_along_axis(line, low, axis=1, mode="promise_in_bounds"),
                total,
            )

        picked = lax.fori_loop(
            0, table_ref.shape[0], body, jnp.ones((step, LANE), F32), unroll=4
        )
        out_ref[first : first + step, :] = 1.0 / picked


def forward_kernel(
    block, segment_rows, member_rows, templates, scale,
    packed_ref, f1_ref, twist_ref, f2_ref, amp_ref, chirp_ref,
    re_ref, im_ref, sigma_ref,
    x_ref, f1_buf, y_buf, f2_buf, weight_ref,
):
    step = pl.program_id(0)
    groups = packed_ref.shape[0]
    depth = re_ref.shape[1]
    coarse2 = depth // FINE
    f1_coarse = f1_ref.shape[1] - FINE
    twist_coarse = twist_ref.shape[1] - FINE

    @pl.when(step == 0)
    def _():
        for j in range(groups):
            high, low = halves(packed_ref[j, :segment_rows, :])
            x_ref[0, :, j * LANE : (j + 1) * LANE] = high
            x_ref[1, :, j * LANE : (j + 1) * LANE] = low

        @pl.loop(0, coarse2)
        def _(outer):
            c, s = product_rows(f2_ref, outer, coarse2)
            put_factor(f2_buf, (pl.ds(pl.multiple_of(outer * FINE, FINE), FINE),), c, s)

        sigma_ref[...] = jnp.zeros_like(sigma_ref)

    per_block = block // FINE

    @pl.loop(0, per_block)
    def _(i):
        rows = (pl.ds(pl.multiple_of(i * FINE, FINE), FINE),)
        c, s = product_rows(f1_ref, step * per_block + i, f1_coarse)
        put(f1_buf, 0, rows, c)
        put(f1_buf, 1, rows, s)

    def real_dot(slot):
        def one(i, j):
            return lax.dot_general(f1_buf[slot, i], x_ref[j], NN, preferred_element_type=F32)

        return one(0, 0) + (one(0, 1) + one(1, 0))

    y_re = real_dot(0)
    y_im = real_dot(1)
    for i in range(per_block):
        span = slice(i * FINE, (i + 1) * FINE)
        c, s = product_rows(twist_ref, step * per_block + i, twist_coarse)
        a, b = y_re[span], y_im[span]
        re = a * c - b * s
        im = a * s + b * c
        put(y_buf, 0, (span,), re + im)
        put(y_buf, 1, (span,), re)
        put(y_buf, 2, (span,), im)
    x_re, x_im = complex_dot(f2_buf, y_buf, NT)

    bands = (packed_ref.shape[1] - segment_rows) // member_rows // (re_ref.shape[2] * 2 // LANE)
    quarters = block // LANE
    all_quarters = (packed_ref.shape[1] - segment_rows) // (member_rows * bands)
    for q in range(quarters):
        lanes = slice(q * LANE, (q + 1) * LANE)
        for band in range(bands):
            for j in range(groups):
                source = segment_rows + ((step * quarters + q) * bands + band) * member_rows
                target = (band * groups + j) * member_rows
                weight_ref[target : target + member_rows, lanes] = packed_ref[
                    j, pl.ds(pl.multiple_of(source, 8), member_rows), :
                ]
    amp = amp_ref[...]
    weight = amp * weight_ref[...]
    sigma_ref[...] += jnp.sum((weight * amp).reshape(-1, 8, block), axis=0)
    weight = weight * scale
    x_re = x_re * weight
    x_im = x_im * weight
    coarse = depth // COARSE
    for m in range(templates):
        c0 = chirp_ref[m, 0, coarse:, :]
        s0 = chirp_ref[m, 1, coarse:, :]
        for i in range(coarse):
            span = slice(i * COARSE, (i + 1) * COARSE)
            c1 = chirp_ref[m, 0, i : i + 1, :]
            s1 = chirp_ref[m, 1, i : i + 1, :]
            c = c1 * c0 - s1 * s0
            s = s1 * c0 + c1 * s0
            a, b = x_re[span], x_im[span]
            re_ref[m, span, :] = a * c - b * s
            im_ref[m, span, :] = a * s + b * c


def inverse_kernel(
    block, templates,
    re_ref, im_ref, i1_ref, twist_ref, i2_ref, sigma_ref,
    out_ref,
    c_buf, i1_buf, i2_buf, g_buf,
):
    step = pl.program_id(0)
    inner = re_ref.shape[2]
    depth = re_ref.shape[1]
    half = i2_buf.shape[2]
    i1_coarse = i1_ref.shape[1] - FINE
    i2_coarse = i2_ref.shape[1] - FINE
    twist_coarse = twist_ref.shape[1] - FINE

    @pl.when(step == 0)
    def _():
        for m in range(templates):
            lanes = slice(m * inner, (m + 1) * inner)
            for first in range(0, depth, COARSE):
                rows = slice(first, first + COARSE)
                re = re_ref[m, rows, :]
                im = im_ref[m, rows, :]
                put(c_buf, 0, (rows, lanes), re + im)
                put(c_buf, 1, (rows, lanes), re)
                put(c_buf, 2, (rows, lanes), im)

        @pl.loop(0, i2_coarse)
        def _(outer):
            c, s = product_rows(i2_ref, outer, i2_coarse)
            put_factor(i2_buf, (pl.ds(pl.multiple_of(outer * FINE, FINE), FINE),), c, s)

    per_block = block // FINE

    @pl.loop(0, per_block)
    def _(i):
        rows = (pl.ds(pl.multiple_of(i * FINE, FINE), FINE),)
        c, s = product_rows(i1_ref, step * per_block + i, i1_coarse)
        put_factor(i1_buf, rows, c, s)

    total = jnp.sum(jnp.sum(sigma_ref[...], axis=0, keepdims=True), axis=1, keepdims=True)
    norm = 1.0 / jnp.sqrt(total)
    g_re, g_im = complex_dot(i1_buf, c_buf, NN)
    quarters = block // LANE
    row_stride = templates * (i1_coarse * FINE // LANE)
    for i in range(per_block):
        span = slice(i * FINE, (i + 1) * FINE)
        c, s = product_rows(twist_ref, step * per_block + i, twist_coarse)
        for m in range(templates):
            lanes = slice(m * inner, (m + 1) * inner)
            a, b = g_re[span, lanes], g_im[span, lanes]
            re = a * c - b * s
            im = a * s + b * c
            put(g_buf.at[m], 0, (span,), re + im)
            put(g_buf.at[m], 1, (span,), re)
            put(g_buf.at[m], 2, (span,), im)
    for m in range(templates):
        z_re, z_im = complex_dot(i2_buf, g_buf.at[m], NT)
        size = jnp.sqrt(z_re * z_re + z_im * z_im) * norm
        for q in range(quarters):
            first = (step * quarters + q) * templates + m
            out_ref[pl.ds(first, half, stride=row_stride), :] = size[:, q * LANE : (q + 1) * LANE]


def local(strain, psd_bins, psd_values, chirp_slope, chirp_curve):
    groups = lax.axis_size("tmpl")
    own_part = strain[0]
    half_len = own_part.shape[0]
    sub_len = 2 * half_len
    total_len = sub_len * groups
    inner = sub_len // LANE
    outer = total_len // inner
    depth = 3 * outer // 8
    k_low = total_len // 200
    k_cut = 3 * total_len // 8
    bands = 3 * groups // 8
    templates = chirp_slope.shape[0]
    member_len = psd_bins.shape[1]
    member_rows = member_len // inner
    assert (COARSE * inner) ** 2 % total_len == 0 and 2 * COARSE * inner**2 % total_len == 0
    assert total_len & (total_len - 1) == 0

    tail = shifted(own_part, "tm", 1)
    bins = psd_bins[:bands].reshape(bands, member_rows, inner // LANE, LANE)
    bins = jnp.transpose(bins, (2, 0, 1, 3)).reshape(-1, LANE)
    inv_psd = pl.pallas_call(
        inverse_density,
        out_shape=jax.ShapeDtypeStruct(bins.shape, F32),
        name="inverse_density",
    )(bins, psd_values[0].reshape(-1, LANE))
    packed = jnp.concatenate(
        [tail.reshape(-1, LANE), own_part.reshape(-1, LANE), inv_psd], axis=0
    )
    packed = lax.all_gather(packed, "tmpl", axis=0, tiled=False)

    place = np.arange(outer)
    sample = (place % LANE) * groups + place // LANE
    f1 = base_table(inner, np.arange(inner), inner, -1.0)
    twist1 = base_table(inner, sample, total_len, -1.0)
    f2 = base_table(depth, sample, outer, -1.0)
    i1 = base_table(outer, np.arange(depth), outer, 1.0)
    twist2 = base_table(outer, np.arange(inner), total_len, 1.0)
    i2 = base_table(inner // 2, np.arange(inner), inner, 1.0, inner // 2)

    frequency = (
        jnp.arange(depth, dtype=jnp.int32)[:, None] * inner
        + jnp.arange(inner, dtype=jnp.int32)[None, :]
    )
    ratio = frequency.astype(F32) / k_low
    inside = (frequency >= k_low) & (frequency < k_cut)
    amplitude = jnp.where(inside, jnp.power(jnp.maximum(ratio, 1.0), -7.0 / 6.0), 0.0)

    slope = chirp_slope[:, None, None]
    curve = chirp_curve[:, None, None]
    column = jnp.arange(inner, dtype=jnp.int32)[None, None, :]
    jump = COARSE * inner * jnp.arange(depth // COARSE, dtype=jnp.int32)[None, :, None]
    near = inner * jnp.arange(COARSE, dtype=jnp.int32)[None, :, None] + column
    mask = total_len - 1
    far_phase = slope * jump + curve * ((2 * jump * column) & mask)
    near_phase = slope * near + curve * ((near * near) & mask)
    phase = jnp.concatenate([far_phase, near_phase], axis=1) & mask
    angle = phase.astype(F32) * (TWO_PI / total_len)
    chirp = jnp.stack([jnp.cos(angle), jnp.sin(angle)], axis=1)

    block = 2 * LANE
    whole = lambda *shape: pl.BlockSpec(shape, lambda i: (0,) * len(shape))
    full = lambda array: whole(*array.shape)
    coef_re, coef_im, sigma = pl.pallas_call(
        functools.partial(
            forward_kernel, block, inner, member_rows, templates, 1.0 / math.sqrt(total_len)
        ),
        grid=(inner // block,),
        in_specs=[
            full(packed), full(f1), full(twist1), full(f2),
            pl.BlockSpec((depth, block), lambda i: (0, i)),
            pl.BlockSpec((templates, 2, chirp.shape[2], block), lambda i: (0, 0, 0, i)),
        ],
        out_specs=[
            pl.BlockSpec((templates, depth, block), lambda i: (0, 0, i)),
            pl.BlockSpec((templates, depth, block), lambda i: (0, 0, i)),
            whole(8, block),
        ],
        out_shape=[
            jax.ShapeDtypeStruct((templates, depth, inner), F32),
            jax.ShapeDtypeStruct((templates, depth, inner), F32),
            jax.ShapeDtypeStruct((8, block), F32),
        ],
        scratch_shapes=[
            pltpu.VMEM((2, inner, outer), BF16),
            pltpu.VMEM((2, 2, block, inner), BF16),
            pltpu.VMEM((3, 2, block, outer), BF16),
            pltpu.VMEM((3, 2, depth, outer), BF16),
            pltpu.VMEM((depth, block), F32),
        ],
        compiler_params=pltpu.CompilerParams(vmem_limit_bytes=VMEM_LIMIT),
        name="forward",
    )(packed, f1, twist1, f2, amplitude, chirp)

    half = inner // 2
    rows = half * (outer // LANE) * templates
    flat = pl.pallas_call(
        functools.partial(inverse_kernel, block, templates),
        grid=(outer // block,),
        in_specs=[
            full(coef_re), full(coef_im), full(i1), full(twist2), full(i2), full(sigma),
        ],
        out_specs=whole(rows, LANE),
        out_shape=jax.ShapeDtypeStruct((rows, LANE), F32),
        scratch_shapes=[
            pltpu.VMEM((3, 2, depth, templates * inner), BF16),
            pltpu.VMEM((3, 2, block, depth), BF16),
            pltpu.VMEM((3, 2, half, inner), BF16),
            pltpu.VMEM((templates, 3, 2, block, inner), BF16),
        ],
        compiler_params=pltpu.CompilerParams(vmem_limit_bytes=VMEM_LIMIT),
        name="inverse",
    )(coef_re, coef_im, i1, twist2, i2, sigma)
    result = flat.reshape(-1, templates, LANE)
    return jnp.transpose(result, (1, 0, 2)).reshape(templates, -1)


def solution(mesh):
    placed = (P("tmpl", "tm"), P(None, "tmpl"), P("tm", None), P("tmpl"), P("tmpl"))
    return jax.shard_map(
        local, mesh=mesh, in_specs=placed, out_specs=P("tmpl", "tm"), check_vma=False
    )
```

```python
import functools
import math

import jax
import jax.numpy as jnp
import numpy as np
from jax import lax
from jax.experimental import pallas as pl
from jax.experimental.pallas import tpu as pltpu
from jax.sharding import PartitionSpec as P

TWO_PI = 2.0 * math.pi
LANE = 128
FINE = 32
COARSE = 16
VMEM_LIMIT = 60 * 1024 * 1024
BF16 = jnp.bfloat16
F32 = jnp.float32
NN = (((1,), (0,)), ((), ()))
NT = (((1,), (1,)), ((), ()))


def shifted(block, axis, distance):
    devices = range(lax.axis_size(axis))
    route = [(i - distance, i) for i in devices if i - distance in devices]
    return lax.ppermute(block, axis, route)


def base_table(rows, cols, modulus, direction, start=0):
    first = start + FINE * np.arange(rows // FINE, dtype=np.int64)
    index = np.concatenate([first, np.arange(FINE, dtype=np.int64)])
    angle = (index[:, None] * np.asarray(cols, dtype=np.int64)[None, :] % modulus) * (
        direction * TWO_PI / modulus
    )
    return jnp.asarray(np.stack([np.cos(angle), np.sin(angle)]).astype(np.float32))


def product_rows(table, outer, coarse_count):
    c1 = table[0, pl.ds(outer, 1), :]
    s1 = table[1, pl.ds(outer, 1), :]
    c0 = table[0, coarse_count : coarse_count + FINE, :]
    s0 = table[1, coarse_count : coarse_count + FINE, :]
    return c1 * c0 - s1 * s0, s1 * c0 + c1 * s0


def halves(value):
    high = value.astype(BF16)
    return high, (value - high.astype(F32)).astype(BF16)


def put(ref, slot, index, value):
    high, low = halves(value)
    ref[(slot, 0) + index] = high
    ref[(slot, 1) + index] = low


def put_factor(ref, index, re, im):
    put(ref, 0, index, re)
    put(ref, 1, index, im - re)
    put(ref, 2, index, re + im)


def dot3(a, b, slot, dims):
    def one(i, j):
        return lax.dot_general(a[slot, i], b[slot, j], dims, preferred_element_type=F32)

    return one(0, 0) + (one(0, 1) + one(1, 0))


def complex_dot(a, b, dims):
    k1 = dot3(a, b, 0, dims)
    k2 = dot3(a, b, 1, dims)
    k3 = dot3(a, b, 2, dims)
    return k1 - k3, k1 + k2


def look_up(bins, table_ref):
    high = bins // LANE
    low = bins % LANE

    def body(row, total):
        lanes = pl.ds(pl.multiple_of(row * LANE, LANE), LANE)
        line = jnp.broadcast_to(table_ref[:, lanes], bins.shape)
        return jnp.where(
            high == row,
            jnp.take_along_axis(line, low, axis=1, mode="promise_in_bounds"),
            total,
        )

    picked = lax.fori_loop(
        0, table_ref.shape[1] // LANE, body, jnp.ones(bins.shape, F32), unroll=4
    )
    return 1.0 / picked


def density_rows(bins_ref, ordered_ref, bands, inner):
    member_rows = bins_ref.shape[1] // inner
    for q in range(inner // LANE):
        for band in range(bands):
            for row in range(member_rows):
                start = row * inner + q * LANE
                target = (q * bands + band) * member_rows + row
                ordered_ref[target : target + 1, :] = bins_ref[
                    band : band + 1, start : start + LANE
                ]


def density_kernel(bands, inner, bins_ref, table_ref, out_ref, ordered_ref):
    density_rows(bins_ref, ordered_ref, bands, inner)
    out_ref[...] = look_up(ordered_ref[...], table_ref)


def amplitude_rows(first, shape, total_len):
    k_low = total_len // 200
    k_cut = 3 * total_len // 8
    row = first + lax.broadcasted_iota(jnp.int32, shape, 0)
    frequency = row * shape[1] + lax.broadcasted_iota(jnp.int32, shape, 1)
    ratio = jnp.maximum(frequency.astype(F32) / k_low, 1.0)
    inside = (frequency >= k_low) & (frequency < k_cut)
    return jnp.where(inside, jnp.exp(jnp.log(ratio) * (-7.0 / 6.0)), 0.0)


def template_rows(slope_ref, curve_ref, chirp_ref, m, total_len):
    inner = chirp_ref.shape[3]
    coarse = chirp_ref.shape[2] - COARSE
    for first in range(0, coarse + COARSE, 8):
        slope = slope_ref[m]
        curve = curve_ref[m]
        if first < coarse:
            row = first
            jump = COARSE * inner
        else:
            row = first - coarse
            jump = 0
        shape = (8, inner)
        index = row + lax.broadcasted_iota(jnp.int32, shape, 0)
        column = lax.broadcasted_iota(jnp.int32, shape, 1)
        mask = total_len - 1
        if jump:
            far = jump * index
            phase = slope * far + curve * ((2 * far * column) & mask)
        else:
            near = inner * index + column
            phase = slope * near + curve * ((near * near) & mask)
        angle = (phase & mask).astype(F32) * (TWO_PI / total_len)
        chirp_ref[m, 0, first : first + 8, :] = jnp.cos(angle)
        chirp_ref[m, 1, first : first + 8, :] = jnp.sin(angle)


def amplitude_table(amp_ref, total_len):
    depth, inner = amp_ref.shape

    @pl.loop(0, depth // 8)
    def _(i):
        first = pl.multiple_of(i * 8, 8)
        amp_ref[pl.ds(first, 8), :] = amplitude_rows(first, (8, inner), total_len)


def table_kernel(total_len, slope_ref, curve_ref, chirp_ref, amp_ref):
    for m in range(chirp_ref.shape[0]):
        template_rows(slope_ref, curve_ref, chirp_ref, m, total_len)
    amplitude_table(amp_ref, total_len)


def gather_kernel(
    bands, inner, total_len,
    own_ref, bins_ref, table_ref, slope_ref, curve_ref,
    out_ref, chirp_ref, amp_ref,
    ordered_ref, send_sem, recv_sem, tail_send, tail_recv,
):
    tm = lax.axis_index("tm")
    me = lax.axis_index("tmpl")
    count = lax.axis_size("tm")
    half = own_ref.shape[0]
    extra = ordered_ref.shape[0]

    def peer(distance):
        low = me % (2 * distance)
        return me - low + (low + distance) % (2 * distance)

    core = peer(1)
    side = peer(2)
    front = peer(4)
    side_front = side + front - me
    spans = ((half, half), (0, half), (2 * half, extra))

    barrier = pltpu.get_barrier_semaphore()
    for other in (core, side, front):
        pl.semaphore_signal(
            barrier, inc=1, device_id={"tmpl": other}, device_id_type=pl.DeviceIdType.MESH
        )

    for other in ((tm + 1) % count, (tm + count - 1) % count):
        pl.semaphore_signal(
            barrier, inc=1, device_id={"tm": other}, device_id_type=pl.DeviceIdType.MESH
        )
    pl.semaphore_wait(barrier, 5)

    def copy(part, kind, slot, piece, target, source=None):
        first, rows = spans[part]
        if piece is not None:
            rows = rows // 2
            first = first + piece * rows
        view = out_ref.at[slot, pl.ds(first, rows), :]
        return pltpu.make_async_remote_copy(
            src_ref=view if source is None else source,
            dst_ref=view,
            send_sem=send_sem.at[part, kind],
            recv_sem=recv_sem.at[part, kind],
            device_id={"tmpl": target},
            device_id_type=pl.DeviceIdType.MESH,
        )

    def send(part, kind, source=None):
        slot, piece, target = (
            (me, None, core), (me, None, side), (me, None, front),
            (side, None, core), (front, None, core),
            (side, 0, front), (front, 1, side),
            (side_front, 0, core), (side_front, 1, core),
        )[kind]
        return copy(part, kind, slot, piece, target, source if kind < 3 else None)

    def first_stage(part, source=None):
        send(part, 1, source).start()
        send(part, 2, source).start()
        send(part, 0, source).start()

    def second_stage(part):
        copy(part, 1, side, None, side).wait_recv()
        send(part, 5).start()
        copy(part, 2, front, None, front).wait_recv()
        send(part, 6).start()
        send(part, 3).start()
        send(part, 4).start()

    def third_stage(part):
        copy(part, 5, side_front, 0, front).wait_recv()
        send(part, 7).start()
        copy(part, 6, side_front, 1, side).wait_recv()
        send(part, 8).start()

    def last_stage(part, source=None):
        other = core + side - me
        across = core + front - me
        corner = core + side_front - me
        copy(part, 0, core, None, core).wait_recv()
        copy(part, 3, other, None, core).wait_recv()
        copy(part, 4, across, None, core).wait_recv()
        copy(part, 7, corner, 0, core).wait_recv()
        copy(part, 8, corner, 1, core).wait_recv()
        for kind in range(9):
            send(part, kind, source).wait_send()

    tail_view = out_ref.at[me, pl.ds(0, half), :]
    tail = pltpu.make_async_remote_copy(
        src_ref=own_ref,
        dst_ref=tail_view,
        send_sem=tail_send,
        recv_sem=tail_recv,
        device_id={"tm": (tm + 1) % count},
        device_id_type=pl.DeviceIdType.MESH,
    )

    @pl.when(tm < count - 1)
    def _():
        tail.start()

    first_stage(0, own_ref)
    out_ref[me, half : 2 * half, :] = own_ref[...]
    density_rows(bins_ref, ordered_ref, bands, inner)
    third = extra // 3

    def densities(i):
        rows = slice(i * third, (i + 1) * third)
        out_ref[me, 2 * half + i * third : 2 * half + (i + 1) * third, :] = look_up(
            ordered_ref[rows, :], table_ref
        )

    @pl.when(tm == 0)
    def _():
        for slot in range(out_ref.shape[0]):
            out_ref[slot, :half, :] = jnp.zeros((half, LANE), F32)

    @pl.when(tm > 0)
    def _():
        tail.wait_recv()
        first_stage(1)

    densities(0)
    second_stage(0)
    densities(1)
    densities(2)
    first_stage(2)
    third_stage(0)

    @pl.when(tm > 0)
    def _():
        second_stage(1)

    template_rows(slope_ref, curve_ref, chirp_ref, 0, total_len)

    @pl.when(tm > 0)
    def _():
        third_stage(1)

    second_stage(2)
    for m in range(1, chirp_ref.shape[0]):
        template_rows(slope_ref, curve_ref, chirp_ref, m, total_len)
    third_stage(2)
    amplitude_table(amp_ref, total_len)
    last_stage(0, own_ref)

    @pl.when(tm > 0)
    def _():
        last_stage(1)

    last_stage(2)

    @pl.when(tm < count - 1)
    def _():
        tail.wait_send()


def forward_kernel(
    block, segment_rows, member_rows, templates, scale,
    packed_ref, f1_ref, twist_ref, f2_ref, amp_ref, chirp_ref,
    re_ref, im_ref, sigma_ref,
    x_ref, f1_buf, y_buf, f2_buf, weight_ref,
):
    step = pl.program_id(0)
    groups = packed_ref.shape[0]
    depth = re_ref.shape[1]
    coarse2 = depth // FINE
    f1_coarse = f1_ref.shape[1] - FINE
    twist_coarse = twist_ref.shape[1] - FINE

    @pl.when(step == 0)
    def _():
        for j in range(groups):
            high, low = halves(packed_ref[j, :segment_rows, :])
            x_ref[0, :, j * LANE : (j + 1) * LANE] = high
            x_ref[1, :, j * LANE : (j + 1) * LANE] = low

        @pl.loop(0, coarse2)
        def _(outer):
            c, s = product_rows(f2_ref, outer, coarse2)
            put_factor(f2_buf, (pl.ds(pl.multiple_of(outer * FINE, FINE), FINE),), c, s)

        sigma_ref[...] = jnp.zeros_like(sigma_ref)

    per_block = block // FINE

    @pl.loop(0, per_block)
    def _(i):
        rows = (pl.ds(pl.multiple_of(i * FINE, FINE), FINE),)
        c, s = product_rows(f1_ref, step * per_block + i, f1_coarse)
        put(f1_buf, 0, rows, c)
        put(f1_buf, 1, rows, s)

    def real_dot(slot):
        def one(i, j):
            return lax.dot_general(f1_buf[slot, i], x_ref[j], NN, preferred_element_type=F32)

        return one(0, 0) + (one(0, 1) + one(1, 0))

    y_re = real_dot(0)
    y_im = real_dot(1)
    for i in range(per_block):
        span = slice(i * FINE, (i + 1) * FINE)
        c, s = product_rows(twist_ref, step * per_block + i, twist_coarse)
        a, b = y_re[span], y_im[span]
        re = a * c - b * s
        im = a * s + b * c
        put(y_buf, 0, (span,), re + im)
        put(y_buf, 1, (span,), re)
        put(y_buf, 2, (span,), im)
    x_re, x_im = complex_dot(f2_buf, y_buf, NT)

    bands = (packed_ref.shape[1] - segment_rows) // member_rows // (re_ref.shape[2] * 2 // LANE)
    quarters = block // LANE
    all_quarters = (packed_ref.shape[1] - segment_rows) // (member_rows * bands)
    for q in range(quarters):
        lanes = slice(q * LANE, (q + 1) * LANE)
        for band in range(bands):
            for j in range(groups):
                source = segment_rows + ((step * quarters + q) * bands + band) * member_rows
                target = (band * groups + j) * member_rows
                weight_ref[target : target + member_rows, lanes] = packed_ref[
                    j, pl.ds(pl.multiple_of(source, 8), member_rows), :
                ]
    amp = amp_ref[...]
    weight = amp * weight_ref[...]
    sigma_ref[...] += jnp.sum((weight * amp).reshape(-1, 8, block), axis=0)
    weight = weight * scale
    x_re = x_re * weight
    x_im = x_im * weight
    coarse = depth // COARSE
    for m in range(templates):
        c0 = chirp_ref[m, 0, coarse:, :]
        s0 = chirp_ref[m, 1, coarse:, :]
        for i in range(coarse):
            span = slice(i * COARSE, (i + 1) * COARSE)
            c1 = chirp_ref[m, 0, i : i + 1, :]
            s1 = chirp_ref[m, 1, i : i + 1, :]
            c = c1 * c0 - s1 * s0
            s = s1 * c0 + c1 * s0
            a, b = x_re[span], x_im[span]
            re_ref[m, span, :] = a * c - b * s
            im_ref[m, span, :] = a * s + b * c


def inverse_kernel(
    block, templates,
    re_ref, im_ref, i1_ref, twist_ref, i2_ref, sigma_ref,
    out_ref,
    c_buf, i1_buf, i2_buf, g_buf,
):
    step = pl.program_id(0)
    inner = re_ref.shape[2]
    depth = re_ref.shape[1]
    half = i2_buf.shape[2]
    i1_coarse = i1_ref.shape[1] - FINE
    i2_coarse = i2_ref.shape[1] - FINE
    twist_coarse = twist_ref.shape[1] - FINE

    @pl.when(step == 0)
    def _():
        for m in range(templates):
            lanes = slice(m * inner, (m + 1) * inner)
            for first in range(0, depth, COARSE):
                rows = slice(first, first + COARSE)
                re = re_ref[m, rows, :]
                im = im_ref[m, rows, :]
                put(c_buf, 0, (rows, lanes), re + im)
                put(c_buf, 1, (rows, lanes), re)
                put(c_buf, 2, (rows, lanes), im)

        @pl.loop(0, i2_coarse)
        def _(outer):
            c, s = product_rows(i2_ref, outer, i2_coarse)
            put_factor(i2_buf, (pl.ds(pl.multiple_of(outer * FINE, FINE), FINE),), c, s)

    per_block = block // FINE

    @pl.loop(0, per_block)
    def _(i):
        rows = (pl.ds(pl.multiple_of(i * FINE, FINE), FINE),)
        c, s = product_rows(i1_ref, step * per_block + i, i1_coarse)
        put_factor(i1_buf, rows, c, s)

    total = jnp.sum(jnp.sum(sigma_ref[...], axis=0, keepdims=True), axis=1, keepdims=True)
    norm = 1.0 / jnp.sqrt(total)
    g_re, g_im = complex_dot(i1_buf, c_buf, NN)
    quarters = block // LANE
    row_stride = templates * (i1_coarse * FINE // LANE)
    for i in range(per_block):
        span = slice(i * FINE, (i + 1) * FINE)
        c, s = product_rows(twist_ref, step * per_block + i, twist_coarse)
        for m in range(templates):
            lanes = slice(m * inner, (m + 1) * inner)
            a, b = g_re[span, lanes], g_im[span, lanes]
            re = a * c - b * s
            im = a * s + b * c
            put(g_buf.at[m], 0, (span,), re + im)
            put(g_buf.at[m], 1, (span,), re)
            put(g_buf.at[m], 2, (span,), im)
    for m in range(templates):
        z_re, z_im = complex_dot(i2_buf, g_buf.at[m], NT)
        size = jnp.sqrt(z_re * z_re + z_im * z_im) * norm
        for q in range(quarters):
            first = (step * quarters + q) * templates + m
            out_ref[pl.ds(first, half, stride=row_stride), :] = size[:, q * LANE : (q + 1) * LANE]


def local(strain, psd_bins, psd_values, chirp_slope, chirp_curve):
    groups = lax.axis_size("tmpl")
    own_part = strain[0]
    half_len = own_part.shape[0]
    sub_len = 2 * half_len
    total_len = sub_len * groups
    inner = sub_len // LANE
    outer = total_len // inner
    depth = 3 * outer // 8
    k_low = total_len // 200
    k_cut = 3 * total_len // 8
    bands = 3 * groups // 8
    templates = chirp_slope.shape[0]
    member_len = psd_bins.shape[1]
    member_rows = member_len // inner
    assert (COARSE * inner) ** 2 % total_len == 0 and 2 * COARSE * inner**2 % total_len == 0
    assert total_len & (total_len - 1) == 0

    extra = bands * member_len // LANE
    table_shapes = [
        jax.ShapeDtypeStruct((templates, 2, depth // COARSE + COARSE, inner), F32),
        jax.ShapeDtypeStruct((depth, inner), F32),
    ]
    vmem = pl.BlockSpec(memory_space=pltpu.VMEM)
    smem = pl.BlockSpec(memory_space=pltpu.SMEM)
    own_rows = own_part.reshape(-1, LANE)
    rows = 2 * own_rows.shape[0] + extra
    if groups == 8:
        packed, chirp, amplitude = pl.pallas_call(
            functools.partial(gather_kernel, bands, inner, total_len),
            in_specs=[vmem, vmem, vmem, smem, smem],
            out_specs=[vmem, vmem, vmem],
            out_shape=[jax.ShapeDtypeStruct((groups, rows, LANE), F32)] + table_shapes,
            scratch_shapes=[
                pltpu.VMEM((extra, LANE), jnp.int32),
                pltpu.SemaphoreType.DMA((3, 9)),
                pltpu.SemaphoreType.DMA((3, 9)),
                pltpu.SemaphoreType.DMA,
                pltpu.SemaphoreType.DMA,
            ],
            compiler_params=pltpu.CompilerParams(collective_id=0, has_side_effects=True),
            name="gather",
        )(own_rows, psd_bins, psd_values, chirp_slope, chirp_curve)
    else:
        tail = shifted(own_part, "tm", 1).reshape(-1, LANE)
        inv_psd = pl.pallas_call(
            functools.partial(density_kernel, bands, inner),
            out_shape=jax.ShapeDtypeStruct((extra, LANE), F32),
            scratch_shapes=[pltpu.VMEM((extra, LANE), jnp.int32)],
            name="density",
        )(psd_bins, psd_values)
        packed = lax.all_gather(
            jnp.concatenate([tail, own_rows, inv_psd], axis=0), "tmpl", axis=0, tiled=False
        )
        chirp, amplitude = pl.pallas_call(
            functools.partial(table_kernel, total_len),
            in_specs=[smem, smem],
            out_shape=table_shapes,
            name="tables",
        )(chirp_slope, chirp_curve)

    place = np.arange(outer)
    sample = (place % LANE) * groups + place // LANE
    f1 = base_table(inner, np.arange(inner), inner, -1.0)
    twist1 = base_table(inner, sample, total_len, -1.0)
    f2 = base_table(depth, sample, outer, -1.0)
    i1 = base_table(outer, np.arange(depth), outer, 1.0)
    twist2 = base_table(outer, np.arange(inner), total_len, 1.0)
    i2 = base_table(inner // 2, np.arange(inner), inner, 1.0, inner // 2)

    block = 2 * LANE
    whole = lambda *shape: pl.BlockSpec(shape, lambda i: (0,) * len(shape))
    full = lambda array: whole(*array.shape)
    coef_re, coef_im, sigma = pl.pallas_call(
        functools.partial(
            forward_kernel, block, inner, member_rows, templates, 1.0 / math.sqrt(total_len)
        ),
        grid=(inner // block,),
        in_specs=[
            full(packed), full(f1), full(twist1), full(f2),
            pl.BlockSpec((depth, block), lambda i: (0, i)),
            pl.BlockSpec((templates, 2, chirp.shape[2], block), lambda i: (0, 0, 0, i)),
        ],
        out_specs=[
            pl.BlockSpec((templates, depth, block), lambda i: (0, 0, i)),
            pl.BlockSpec((templates, depth, block), lambda i: (0, 0, i)),
            whole(8, block),
        ],
        out_shape=[
            jax.ShapeDtypeStruct((templates, depth, inner), F32),
            jax.ShapeDtypeStruct((templates, depth, inner), F32),
            jax.ShapeDtypeStruct((8, block), F32),
        ],
        scratch_shapes=[
            pltpu.VMEM((2, inner, outer), BF16),
            pltpu.VMEM((2, 2, block, inner), BF16),
            pltpu.VMEM((3, 2, block, outer), BF16),
            pltpu.VMEM((3, 2, depth, outer), BF16),
            pltpu.VMEM((depth, block), F32),
        ],
        compiler_params=pltpu.CompilerParams(vmem_limit_bytes=VMEM_LIMIT),
        name="forward",
    )(packed, f1, twist1, f2, amplitude, chirp)

    half = inner // 2
    rows = half * (outer // LANE) * templates
    flat = pl.pallas_call(
        functools.partial(inverse_kernel, block, templates),
        grid=(outer // block,),
        in_specs=[
            full(coef_re), full(coef_im), full(i1), full(twist2), full(i2), full(sigma),
        ],
        out_specs=whole(rows, LANE),
        out_shape=jax.ShapeDtypeStruct((rows, LANE), F32),
        scratch_shapes=[
            pltpu.VMEM((3, 2, depth, templates * inner), BF16),
            pltpu.VMEM((3, 2, block, depth), BF16),
            pltpu.VMEM((3, 2, half, inner), BF16),
            pltpu.VMEM((templates, 3, 2, block, inner), BF16),
        ],
        compiler_params=pltpu.CompilerParams(vmem_limit_bytes=VMEM_LIMIT),
        name="inverse",
    )(coef_re, coef_im, i1, twist2, i2, sigma)
    result = flat.reshape(-1, templates, LANE)
    return jnp.transpose(result, (1, 0, 2)).reshape(templates, -1)


def solution(mesh):
    placed = (P("tmpl", "tm"), P(None, "tmpl"), P("tm", None), P("tmpl"), P("tmpl"))
    return jax.shard_map(
        local, mesh=mesh, in_specs=placed, out_specs=P("tmpl", "tm"), check_vma=False
    )
```

```python
import functools
import math

import jax
import jax.numpy as jnp
import numpy as np
from jax import lax
from jax.experimental import pallas as pl
from jax.experimental.pallas import tpu as pltpu
from jax.sharding import PartitionSpec as P

TWO_PI = 2.0 * math.pi
LANE = 128
FINE = 32
COARSE = 16
VMEM_LIMIT = 60 * 1024 * 1024
BF16 = jnp.bfloat16
F32 = jnp.float32
NN = (((1,), (0,)), ((), ()))
NT = (((1,), (1,)), ((), ()))


def shifted(block, axis, distance):
    devices = range(lax.axis_size(axis))
    route = [(i - distance, i) for i in devices if i - distance in devices]
    return lax.ppermute(block, axis, route)


def base_table(rows, cols, modulus, direction, start=0):
    first = start + FINE * np.arange(rows // FINE, dtype=np.int64)
    index = np.concatenate([first, np.arange(FINE, dtype=np.int64)])
    angle = (index[:, None] * np.asarray(cols, dtype=np.int64)[None, :] % modulus) * (
        direction * TWO_PI / modulus
    )
    return jnp.asarray(np.stack([np.cos(angle), np.sin(angle)]).astype(np.float32))


def product_rows(table, outer, coarse_count):
    c1 = table[0, pl.ds(outer, 1), :]
    s1 = table[1, pl.ds(outer, 1), :]
    c0 = table[0, coarse_count : coarse_count + FINE, :]
    s0 = table[1, coarse_count : coarse_count + FINE, :]
    return c1 * c0 - s1 * s0, s1 * c0 + c1 * s0


def halves(value):
    high = value.astype(BF16)
    return high, (value - high.astype(F32)).astype(BF16)


def put(ref, slot, index, value):
    high, low = halves(value)
    ref[(slot, 0) + index] = high
    ref[(slot, 1) + index] = low


def put_factor(ref, index, re, im):
    put(ref, 0, index, re)
    put(ref, 1, index, im - re)
    put(ref, 2, index, re + im)


def split_dot(a_high, a_low, b_high, b_low, dims):
    ((a_axis,), (b_axis,)), _ = dims
    a = jnp.concatenate([a_high, a_low, a_high], axis=a_axis)
    b = jnp.concatenate([b_low, b_high, b_high], axis=b_axis)
    return lax.dot_general(a, b, dims, preferred_element_type=F32)


def dot3(a, b, slot, dims):
    return split_dot(a[slot, 0], a[slot, 1], b[slot, 0], b[slot, 1], dims)


def complex_dot(a, b, dims):
    k1 = dot3(a, b, 0, dims)
    k2 = dot3(a, b, 1, dims)
    k3 = dot3(a, b, 2, dims)
    return k1 - k3, k1 + k2


def look_up(bins, table_ref):
    high = bins // LANE
    low = bins % LANE

    def body(row, total):
        lanes = pl.ds(pl.multiple_of(row * LANE, LANE), LANE)
        line = jnp.broadcast_to(table_ref[:, lanes], bins.shape)
        return jnp.where(
            high == row,
            jnp.take_along_axis(line, low, axis=1, mode="promise_in_bounds"),
            total,
        )

    picked = lax.fori_loop(
        0, table_ref.shape[1] // LANE, body, jnp.ones(bins.shape, F32), unroll=4
    )
    return 1.0 / picked


def density_rows(bins_ref, ordered_ref, bands, inner):
    member_rows = bins_ref.shape[1] // inner
    for q in range(inner // LANE):
        for band in range(bands):
            for row in range(member_rows):
                start = row * inner + q * LANE
                target = (q * bands + band) * member_rows + row
                ordered_ref[target : target + 1, :] = bins_ref[
                    band : band + 1, start : start + LANE
                ]


def density_kernel(bands, inner, bins_ref, table_ref, out_ref, ordered_ref):
    density_rows(bins_ref, ordered_ref, bands, inner)
    out_ref[...] = look_up(ordered_ref[...], table_ref)


def amplitude_rows(first, shape, total_len):
    k_low = total_len // 200
    k_cut = 3 * total_len // 8
    row = first + lax.broadcasted_iota(jnp.int32, shape, 0)
    frequency = row * shape[1] + lax.broadcasted_iota(jnp.int32, shape, 1)
    ratio = jnp.maximum(frequency.astype(F32) / k_low, 1.0)
    inside = (frequency >= k_low) & (frequency < k_cut)
    return jnp.where(inside, jnp.exp(jnp.log(ratio) * (-7.0 / 6.0)), 0.0)


def template_rows(slope_ref, curve_ref, chirp_ref, m, total_len):
    inner = chirp_ref.shape[3]
    coarse = chirp_ref.shape[2] - COARSE
    for first in range(0, coarse + COARSE, 8):
        slope = slope_ref[m]
        curve = curve_ref[m]
        if first < coarse:
            row = first
            jump = COARSE * inner
        else:
            row = first - coarse
            jump = 0
        shape = (8, inner)
        index = row + lax.broadcasted_iota(jnp.int32, shape, 0)
        column = lax.broadcasted_iota(jnp.int32, shape, 1)
        mask = total_len - 1
        if jump:
            far = jump * index
            phase = slope * far + curve * ((2 * far * column) & mask)
        else:
            near = inner * index + column
            phase = slope * near + curve * ((near * near) & mask)
        angle = (phase & mask).astype(F32) * (TWO_PI / total_len)
        chirp_ref[m, 0, first : first + 8, :] = jnp.cos(angle)
        chirp_ref[m, 1, first : first + 8, :] = jnp.sin(angle)


def amplitude_table(amp_ref, total_len):
    depth, inner = amp_ref.shape

    @pl.loop(0, depth // 8)
    def _(i):
        first = pl.multiple_of(i * 8, 8)
        amp_ref[pl.ds(first, 8), :] = amplitude_rows(first, (8, inner), total_len)


def table_kernel(total_len, slope_ref, curve_ref, chirp_ref, amp_ref):
    for m in range(chirp_ref.shape[0]):
        template_rows(slope_ref, curve_ref, chirp_ref, m, total_len)
    amplitude_table(amp_ref, total_len)


def gather_kernel(
    bands, inner, total_len,
    own_ref, bins_ref, table_ref, slope_ref, curve_ref,
    out_ref, chirp_ref, amp_ref,
    ordered_ref, send_sem, recv_sem, tail_send, tail_recv,
):
    tm = lax.axis_index("tm")
    me = lax.axis_index("tmpl")
    count = lax.axis_size("tm")
    half = own_ref.shape[0]
    extra = ordered_ref.shape[0]

    def peer(distance):
        low = me % (2 * distance)
        return me - low + (low + distance) % (2 * distance)

    core = peer(1)
    side = peer(2)
    front = peer(4)
    side_front = side + front - me
    spans = ((half, half), (0, half), (2 * half, extra))

    barrier = pltpu.get_barrier_semaphore()
    for other in (core, side, front):
        pl.semaphore_signal(
            barrier, inc=1, device_id={"tmpl": other}, device_id_type=pl.DeviceIdType.MESH
        )

    for other in ((tm + 1) % count, (tm + count - 1) % count):
        pl.semaphore_signal(
            barrier, inc=1, device_id={"tm": other}, device_id_type=pl.DeviceIdType.MESH
        )
    pl.semaphore_wait(barrier, 5)

    def copy(part, kind, slot, piece, target, source=None):
        first, rows = spans[part]
        if piece is not None:
            rows = rows // 2
            first = first + piece * rows
        view = out_ref.at[slot, pl.ds(first, rows), :]
        return pltpu.make_async_remote_copy(
            src_ref=view if source is None else source,
            dst_ref=view,
            send_sem=send_sem.at[part, kind],
            recv_sem=recv_sem.at[part, kind],
            device_id={"tmpl": target},
            device_id_type=pl.DeviceIdType.MESH,
        )

    def send(part, kind, source=None):
        slot, piece, target = (
            (me, None, core), (me, None, side), (me, None, front),
            (side, None, core), (front, None, core),
            (side, 0, front), (front, 1, side),
            (side_front, 0, core), (side_front, 1, core),
        )[kind]
        return copy(part, kind, slot, piece, target, source if kind < 3 else None)

    def first_stage(part, source=None):
        send(part, 1, source).start()
        send(part, 2, source).start()
        send(part, 0, source).start()

    def second_stage(part):
        copy(part, 1, side, None, side).wait_recv()
        send(part, 5).start()
        copy(part, 2, front, None, front).wait_recv()
        send(part, 6).start()
        send(part, 3).start()
        send(part, 4).start()

    def third_stage(part):
        copy(part, 5, side_front, 0, front).wait_recv()
        send(part, 7).start()
        copy(part, 6, side_front, 1, side).wait_recv()
        send(part, 8).start()

    def last_stage(part, source=None):
        other = core + side - me
        across = core + front - me
        corner = core + side_front - me
        copy(part, 0, core, None, core).wait_recv()
        copy(part, 3, other, None, core).wait_recv()
        copy(part, 4, across, None, core).wait_recv()
        copy(part, 7, corner, 0, core).wait_recv()
        copy(part, 8, corner, 1, core).wait_recv()
        for kind in range(9):
            send(part, kind, source).wait_send()

    tail_view = out_ref.at[me, pl.ds(0, half), :]
    tail = pltpu.make_async_remote_copy(
        src_ref=own_ref,
        dst_ref=tail_view,
        send_sem=tail_send,
        recv_sem=tail_recv,
        device_id={"tm": (tm + 1) % count},
        device_id_type=pl.DeviceIdType.MESH,
    )

    @pl.when(tm < count - 1)
    def _():
        tail.start()

    first_stage(0, own_ref)
    out_ref[me, half : 2 * half, :] = own_ref[...]
    density_rows(bins_ref, ordered_ref, bands, inner)
    third = extra // 3

    def densities(i):
        rows = slice(i * third, (i + 1) * third)
        out_ref[me, 2 * half + i * third : 2 * half + (i + 1) * third, :] = look_up(
            ordered_ref[rows, :], table_ref
        )

    @pl.when(tm == 0)
    def _():
        for slot in range(out_ref.shape[0]):
            out_ref[slot, :half, :] = jnp.zeros((half, LANE), F32)

    @pl.when(tm > 0)
    def _():
        tail.wait_recv()
        first_stage(1)

    densities(0)
    second_stage(0)
    densities(1)
    densities(2)
    first_stage(2)
    third_stage(0)

    @pl.when(tm > 0)
    def _():
        second_stage(1)

    template_rows(slope_ref, curve_ref, chirp_ref, 0, total_len)

    @pl.when(tm > 0)
    def _():
        third_stage(1)

    second_stage(2)
    for m in range(1, chirp_ref.shape[0]):
        template_rows(slope_ref, curve_ref, chirp_ref, m, total_len)
    third_stage(2)
    amplitude_table(amp_ref, total_len)
    last_stage(0, own_ref)

    @pl.when(tm > 0)
    def _():
        last_stage(1)

    last_stage(2)

    @pl.when(tm < count - 1)
    def _():
        tail.wait_send()


def forward_kernel(
    block, segment_rows, member_rows, templates, scale,
    packed_ref, f1_ref, twist_ref, f2_ref, amp_ref, chirp_ref,
    re_ref, im_ref, sigma_ref,
    x_ref, f1_buf, y_buf, f2_buf, weight_ref,
):
    step = pl.program_id(0)
    groups = packed_ref.shape[0]
    depth = re_ref.shape[1]
    coarse2 = depth // FINE
    f1_coarse = f1_ref.shape[1] - FINE
    twist_coarse = twist_ref.shape[1] - FINE

    @pl.when(step == 0)
    def _():
        for j in range(groups):
            high, low = halves(packed_ref[j, :segment_rows, :])
            x_ref[0, :, j * LANE : (j + 1) * LANE] = high
            x_ref[1, :, j * LANE : (j + 1) * LANE] = low

        @pl.loop(0, coarse2)
        def _(outer):
            c, s = product_rows(f2_ref, outer, coarse2)
            put_factor(f2_buf, (pl.ds(pl.multiple_of(outer * FINE, FINE), FINE),), c, s)

        sigma_ref[...] = jnp.zeros_like(sigma_ref)

    per_block = block // FINE

    @pl.loop(0, per_block)
    def _(i):
        rows = (pl.ds(pl.multiple_of(i * FINE, FINE), FINE),)
        c, s = product_rows(f1_ref, step * per_block + i, f1_coarse)
        put(f1_buf, 0, rows, c)
        put(f1_buf, 1, rows, s)

    def real_dot(slot):
        return split_dot(f1_buf[slot, 0], f1_buf[slot, 1], x_ref[0], x_ref[1], NN)

    y_re = real_dot(0)
    y_im = real_dot(1)
    for i in range(per_block):
        span = slice(i * FINE, (i + 1) * FINE)
        c, s = product_rows(twist_ref, step * per_block + i, twist_coarse)
        a, b = y_re[span], y_im[span]
        re = a * c - b * s
        im = a * s + b * c
        put(y_buf, 0, (span,), re + im)
        put(y_buf, 1, (span,), re)
        put(y_buf, 2, (span,), im)
    x_re, x_im = complex_dot(f2_buf, y_buf, NT)

    bands = (packed_ref.shape[1] - segment_rows) // member_rows // (re_ref.shape[2] * 2 // LANE)
    quarters = block // LANE
    all_quarters = (packed_ref.shape[1] - segment_rows) // (member_rows * bands)
    for q in range(quarters):
        lanes = slice(q * LANE, (q + 1) * LANE)
        for band in range(bands):
            for j in range(groups):
                source = segment_rows + ((step * quarters + q) * bands + band) * member_rows
                target = (band * groups + j) * member_rows
                weight_ref[target : target + member_rows, lanes] = packed_ref[
                    j, pl.ds(pl.multiple_of(source, 8), member_rows), :
                ]
    amp = amp_ref[...]
    weight = amp * weight_ref[...]
    sigma_ref[...] += jnp.sum((weight * amp).reshape(-1, 8, block), axis=0)
    weight = weight * scale
    x_re = x_re * weight
    x_im = x_im * weight
    coarse = depth // COARSE
    for m in range(templates):
        c0 = chirp_ref[m, 0, coarse:, :]
        s0 = chirp_ref[m, 1, coarse:, :]
        for i in range(coarse):
            span = slice(i * COARSE, (i + 1) * COARSE)
            c1 = chirp_ref[m, 0, i : i + 1, :]
            s1 = chirp_ref[m, 1, i : i + 1, :]
            c = c1 * c0 - s1 * s0
            s = s1 * c0 + c1 * s0
            a, b = x_re[span], x_im[span]
            re_ref[m, span, :] = a * c - b * s
            im_ref[m, span, :] = a * s + b * c


def inverse_kernel(
    block, templates,
    re_ref, im_ref, i1_ref, twist_ref, i2_ref, sigma_ref,
    out_ref,
    c_buf, i1_buf, i2_buf, g_buf,
):
    step = pl.program_id(0)
    inner = re_ref.shape[2]
    depth = re_ref.shape[1]
    half = i2_buf.shape[2]
    i1_coarse = i1_ref.shape[1] - FINE
    i2_coarse = i2_ref.shape[1] - FINE
    twist_coarse = twist_ref.shape[1] - FINE

    @pl.when(step == 0)
    def _():
        for m in range(templates):
            lanes = slice(m * inner, (m + 1) * inner)
            for first in range(0, depth, COARSE):
                rows = slice(first, first + COARSE)
                re = re_ref[m, rows, :]
                im = im_ref[m, rows, :]
                put(c_buf, 0, (rows, lanes), re + im)
                put(c_buf, 1, (rows, lanes), re)
                put(c_buf, 2, (rows, lanes), im)

        @pl.loop(0, i2_coarse)
        def _(outer):
            c, s = product_rows(i2_ref, outer, i2_coarse)
            put_factor(i2_buf, (pl.ds(pl.multiple_of(outer * FINE, FINE), FINE),), c, s)

    per_block = block // FINE

    @pl.loop(0, per_block)
    def _(i):
        rows = (pl.ds(pl.multiple_of(i * FINE, FINE), FINE),)
        c, s = product_rows(i1_ref, step * per_block + i, i1_coarse)
        put_factor(i1_buf, rows, c, s)

    total = jnp.sum(jnp.sum(sigma_ref[...], axis=0, keepdims=True), axis=1, keepdims=True)
    norm = 1.0 / jnp.sqrt(total)
    g_re, g_im = complex_dot(i1_buf, c_buf, NN)
    quarters = block // LANE
    row_stride = templates * (i1_coarse * FINE // LANE)
    for i in range(per_block):
        span = slice(i * FINE, (i + 1) * FINE)
        c, s = product_rows(twist_ref, step * per_block + i, twist_coarse)
        for m in range(templates):
            lanes = slice(m * inner, (m + 1) * inner)
            a, b = g_re[span, lanes], g_im[span, lanes]
            re = a * c - b * s
            im = a * s + b * c
            put(g_buf.at[m], 0, (span,), re + im)
            put(g_buf.at[m], 1, (span,), re)
            put(g_buf.at[m], 2, (span,), im)
    for m in range(templates):
        z_re, z_im = complex_dot(i2_buf, g_buf.at[m], NT)
        size = jnp.sqrt(z_re * z_re + z_im * z_im) * norm
        for q in range(quarters):
            first = (step * quarters + q) * templates + m
            out_ref[pl.ds(first, half, stride=row_stride), :] = size[:, q * LANE : (q + 1) * LANE]


def local(strain, psd_bins, psd_values, chirp_slope, chirp_curve):
    groups = lax.axis_size("tmpl")
    own_part = strain[0]
    half_len = own_part.shape[0]
    sub_len = 2 * half_len
    total_len = sub_len * groups
    inner = sub_len // LANE
    outer = total_len // inner
    depth = 3 * outer // 8
    k_low = total_len // 200
    k_cut = 3 * total_len // 8
    bands = 3 * groups // 8
    templates = chirp_slope.shape[0]
    member_len = psd_bins.shape[1]
    member_rows = member_len // inner
    assert (COARSE * inner) ** 2 % total_len == 0 and 2 * COARSE * inner**2 % total_len == 0
    assert total_len & (total_len - 1) == 0

    extra = bands * member_len // LANE
    table_shapes = [
        jax.ShapeDtypeStruct((templates, 2, depth // COARSE + COARSE, inner), F32),
        jax.ShapeDtypeStruct((depth, inner), F32),
    ]
    vmem = pl.BlockSpec(memory_space=pltpu.VMEM)
    smem = pl.BlockSpec(memory_space=pltpu.SMEM)
    own_rows = own_part.reshape(-1, LANE)
    rows = 2 * own_rows.shape[0] + extra
    if groups == 8:
        packed, chirp, amplitude = pl.pallas_call(
            functools.partial(gather_kernel, bands, inner, total_len),
            in_specs=[vmem, vmem, vmem, smem, smem],
            out_specs=[vmem, vmem, vmem],
            out_shape=[jax.ShapeDtypeStruct((groups, rows, LANE), F32)] + table_shapes,
            scratch_shapes=[
                pltpu.VMEM((extra, LANE), jnp.int32),
                pltpu.SemaphoreType.DMA((3, 9)),
                pltpu.SemaphoreType.DMA((3, 9)),
                pltpu.SemaphoreType.DMA,
                pltpu.SemaphoreType.DMA,
            ],
            compiler_params=pltpu.CompilerParams(collective_id=0, has_side_effects=True),
            name="gather",
        )(own_rows, psd_bins, psd_values, chirp_slope, chirp_curve)
    else:
        tail = shifted(own_part, "tm", 1).reshape(-1, LANE)
        inv_psd = pl.pallas_call(
            functools.partial(density_kernel, bands, inner),
            out_shape=jax.ShapeDtypeStruct((extra, LANE), F32),
            scratch_shapes=[pltpu.VMEM((extra, LANE), jnp.int32)],
            name="density",
        )(psd_bins, psd_values)
        packed = lax.all_gather(
            jnp.concatenate([tail, own_rows, inv_psd], axis=0), "tmpl", axis=0, tiled=False
        )
        chirp, amplitude = pl.pallas_call(
            functools.partial(table_kernel, total_len),
            in_specs=[smem, smem],
            out_shape=table_shapes,
            name="tables",
        )(chirp_slope, chirp_curve)

    place = np.arange(outer)
    sample = (place % LANE) * groups + place // LANE
    f1 = base_table(inner, np.arange(inner), inner, -1.0)
    twist1 = base_table(inner, sample, total_len, -1.0)
    f2 = base_table(depth, sample, outer, -1.0)
    i1 = base_table(outer, np.arange(depth), outer, 1.0)
    twist2 = base_table(outer, np.arange(inner), total_len, 1.0)
    i2 = base_table(inner // 2, np.arange(inner), inner, 1.0, inner // 2)

    block = 2 * LANE
    whole = lambda *shape: pl.BlockSpec(shape, lambda i: (0,) * len(shape))
    full = lambda array: whole(*array.shape)
    coef_re, coef_im, sigma = pl.pallas_call(
        functools.partial(
            forward_kernel, block, inner, member_rows, templates, 1.0 / math.sqrt(total_len)
        ),
        grid=(inner // block,),
        in_specs=[
            full(packed), full(f1), full(twist1), full(f2),
            pl.BlockSpec((depth, block), lambda i: (0, i)),
            pl.BlockSpec((templates, 2, chirp.shape[2], block), lambda i: (0, 0, 0, i)),
        ],
        out_specs=[
            pl.BlockSpec((templates, depth, block), lambda i: (0, 0, i)),
            pl.BlockSpec((templates, depth, block), lambda i: (0, 0, i)),
            whole(8, block),
        ],
        out_shape=[
            jax.ShapeDtypeStruct((templates, depth, inner), F32),
            jax.ShapeDtypeStruct((templates, depth, inner), F32),
            jax.ShapeDtypeStruct((8, block), F32),
        ],
        scratch_shapes=[
            pltpu.VMEM((2, inner, outer), BF16),
            pltpu.VMEM((2, 2, block, inner), BF16),
            pltpu.VMEM((3, 2, block, outer), BF16),
            pltpu.VMEM((3, 2, depth, outer), BF16),
            pltpu.VMEM((depth, block), F32),
        ],
        compiler_params=pltpu.CompilerParams(vmem_limit_bytes=VMEM_LIMIT),
        name="forward",
    )(packed, f1, twist1, f2, amplitude, chirp)

    half = inner // 2
    rows = half * (outer // LANE) * templates
    flat = pl.pallas_call(
        functools.partial(inverse_kernel, block, templates),
        grid=(outer // block,),
        in_specs=[
            full(coef_re), full(coef_im), full(i1), full(twist2), full(i2), full(sigma),
        ],
        out_specs=whole(rows, LANE),
        out_shape=jax.ShapeDtypeStruct((rows, LANE), F32),
        scratch_shapes=[
            pltpu.VMEM((3, 2, depth, templates * inner), BF16),
            pltpu.VMEM((3, 2, block, depth), BF16),
            pltpu.VMEM((3, 2, half, inner), BF16),
            pltpu.VMEM((templates, 3, 2, block, inner), BF16),
        ],
        compiler_params=pltpu.CompilerParams(vmem_limit_bytes=VMEM_LIMIT),
        name="inverse",
    )(coef_re, coef_im, i1, twist2, i2, sigma)
    result = flat.reshape(-1, templates, LANE)
    return jnp.transpose(result, (1, 0, 2)).reshape(templates, -1)


def solution(mesh):
    placed = (P("tmpl", "tm"), P(None, "tmpl"), P("tm", None), P("tmpl"), P("tmpl"))
    return jax.shard_map(
        local, mesh=mesh, in_specs=placed, out_specs=P("tmpl", "tm"), check_vma=False
    )
```
